32 devices in a mesh: aa: 8 (over y, x, core), ba: 4 (over z).
Axes of the slice: x: 2, y: 2, z: 4, core: 2. Of those that a mesh axis runs over, the one named last changes fastest.
Arguments:
- cotangent: bfloat16 [1, 20, 64, 64, 2048], P(None, None, 'aa', 'ba'), may hold values from -6 to 6
- pre_activations: bfloat16 [2, 1, 20, 64, 64, 2048], P(None, None, None, 'aa', 'ba'), may hold values from -6 to 6
- spectral_weights: bfloat16 [2, 2, 20, 20, 24, 6912], P(None, None, None, None, 'ba', 'aa'), may hold values from -6 to 6
- skip_weights: bfloat16 [2, 20, 20], replicated, may hold values from -1.25 to 1.25
- lift_weights: float32 [20], replicated, may hold values from -1.25 to 1.25
Outputs:
- perm_grad: float32 [1, 64, 64, 2048], P(None, 'aa', 'ba')
The draws below stay inside these ranges and needn't reach their ends.
All inputs are finite; a program needn't handle non-finite values.
Results may differ from the reference program's by a relative error of at most 0.023.
Values may be sent and summed in bfloat16 or wider, within the bound.
A program may use at most 256 MiB of HBM per device.

```python
import math
import jax
import jax.numpy as jnp
from jax import lax

C = 20
NX = 64
NY = 64
NZ = 64
NT = 32
KX = 24
KY = 24
KZ = 24
KT = 12
LAYERS = 2
B = 1


def level_of(key, extent, cuts, smallest, top_value):
    factor_of = 1.0
    for dim, blocks in cuts:
        steps = jax.random.uniform(jax.random.fold_in(jax.random.fold_in(key, 6), dim), (blocks,), jnp.float32, smallest / len(cuts), top_value / len(cuts))
        factor_of = factor_of * jnp.repeat(jnp.exp(steps), extent[dim] // blocks).reshape((-1,) + (1,) * (len(extent) - 1 - dim))
    return factor_of


def normal_values(key, dims, deviation, reach, pieces=(), kind=jnp.bfloat16):
    entries = deviation * jax.random.normal(key, dims, jnp.float32)
    if pieces:
        entries = entries * level_of(key, dims, pieces, -0.22, 0.18)
    return jnp.clip(entries, -reach, reach).astype(kind)


def setup_inputs(seed: int = 0) -> dict:
    key_of = jax.random.split(jax.random.key(seed), 6)
    return {
        "cotangent": normal_values(key_of[0], (B, C, NX, NY, NZ * NT), 1.0, 6.0, ((2, 8), (3, 4))),
        "pre_activations": normal_values(key_of[1], (LAYERS, B, C, NX, NY, NZ * NT), 1.0, 6.0, ((3, 8), (4, 4))),
        "spectral_weights": normal_values(key_of[2], (LAYERS, 2, C, C, KX, KZ * KT * KY), ((NX * NY * NZ * NT) ** 0.5 * (KX * KY * KZ * KT * C) ** -0.5), 6.0, ((4, 4), (5, 8))),
        "skip_weights": normal_values(key_of[3], (LAYERS, C, C), C ** -0.5, 1.25),
        "lift_weights": normal_values(key_of[4], (C,), C ** -0.5, 1.25, (), jnp.float32),
    }


def gelu_slope(values):
    normal_cdf = 0.5 * (1.0 + lax.erf(values / math.sqrt(2.0)))
    density = jnp.exp(-0.5 * values * values) / math.sqrt(2.0 * math.pi)
    return normal_cdf + values * density

def round_complex(values):
    real_part = lax.optimization_barrier(values.real.astype(jnp.bfloat16)).astype(jnp.float32)
    imag_part = lax.optimization_barrier(values.imag.astype(jnp.bfloat16)).astype(jnp.float32)
    return lax.complex(real_part, imag_part)

def kept_index(total_count, length):
    return jnp.concatenate([jnp.arange(total_count // 2, dtype=jnp.int32), jnp.arange(length - total_count // 2, length, dtype=jnp.int32)])

def forward_field(field):
    values = field.astype(jnp.float32).reshape(NX, NY, NZ, NT)
    spectrum = jnp.fft.fft2(values, axes=(2, 3))
    spectrum = jnp.take(spectrum, kept_index(KZ, NZ), axis=2)
    spectrum = round_complex(spectrum[:, :, :, :KT])
    spectrum = round_complex(jnp.take(jnp.fft.fft(spectrum, axis=0), kept_index(KX, NX), axis=0))
    spectrum = round_complex(jnp.take(jnp.fft.fft(spectrum, axis=1), kept_index(KY, NY), axis=1))
    return spectrum

def inverse_field(mode_values, rounded):
    gridded = jnp.zeros((KX, NY, KZ, KT), mode_values.dtype).at[:, kept_index(KY, NY)].set(mode_values)
    gridded = jnp.fft.ifft(gridded, axis=1)
    if rounded:
        gridded = round_complex(gridded)
    spread = jnp.zeros((NX, NY, KZ, KT), mode_values.dtype).at[kept_index(KX, NX)].set(gridded)
    spread = jnp.fft.ifft(spread, axis=0)
    if rounded:
        spread = round_complex(spread)
    plane = jnp.zeros((NX, NY, NZ, NT), mode_values.dtype).at[:, :, kept_index(KZ, NZ), :KT].set(spread)
    return jnp.fft.ifft2(plane, axes=(2, 3)).real.reshape(NX, NY, NZ * NT)

def mix_modes(spectrum, weights):
    shaped = weights.astype(jnp.float32).reshape(2, C, C, KX, KZ, KT, KY)
    conj_weights = lax.complex(shaped[0], -shaped[1])
    return jnp.einsum('oxyzt,oixzty->ixyzt', spectrum, conj_weights)

def sample_grad(cot_sample, pre_sample, spectral_weights, skip_weights, lift_weights):
    incoming = cot_sample.astype(jnp.float32)
    for level_index in range(LAYERS - 1, -1, -1):
        grad_pre = (incoming * gelu_slope(pre_sample[level_index].astype(jnp.float32))).astype(jnp.bfloat16)
        spectrum = lax.map(forward_field, grad_pre)
        mode_values = mix_modes(spectrum, spectral_weights[level_index])
        if level_index > 0:
            mode_values = round_complex(mode_values)
            spectral = lax.map(lambda entry: inverse_field(entry, True), mode_values)
        else:
            spectral = lax.map(lambda entry: inverse_field(entry, False), mode_values)
        skip_term = jnp.einsum('oxyz,oi->ixyz', grad_pre.astype(jnp.float32), skip_weights[level_index].astype(jnp.float32), precision=lax.Precision.HIGHEST)
        incoming = skip_term + spectral
    return jnp.einsum('cxyz,c->xyz', incoming, lift_weights, precision=lax.Precision.HIGHEST)

def reference(cotangent, pre_activations, spectral_weights, skip_weights, lift_weights):

    def one_sample(sample_index):
        cot_sample = lax.dynamic_index_in_dim(cotangent, sample_index, 0, keepdims=False)
        pre_sample = lax.dynamic_index_in_dim(pre_activations, sample_index, 1, keepdims=False)
        return sample_grad(cot_sample, pre_sample, spectral_weights, skip_weights, lift_weights)
    return lax.map(one_sample, jnp.arange(B, dtype=jnp.int32))
```

```python
import math

import jax
import jax.numpy as jnp
import numpy as np
from jax import lax
from jax.sharding import PartitionSpec as P

NX = 64
NY = 64
NZ = 64
NT = 32
KX = 24
KY = 24
KZ = 24
KT = 12


def gelu_slope(values):
    normal_cdf = 0.5 * (1.0 + lax.erf(values / math.sqrt(2.0)))
    density = jnp.exp(-0.5 * values * values) / math.sqrt(2.0 * math.pi)
    return normal_cdf + values * density


def signed_freq(total_count):
    index_list = np.arange(total_count)
    return np.where(index_list < total_count // 2, index_list, index_list - total_count)


def line_tables(total_count, length):
    turns = signed_freq(total_count)[:, None] * np.arange(length)[None, :] % length
    angles = 2.0 * math.pi / length * turns
    cosine = np.cos(angles)
    sine_part = np.sin(angles)
    forward = np.stack(
        [np.stack([cosine.T, -sine_part.T], 1), np.stack([sine_part.T, cosine.T], 1)], 0
    )
    inverse = (
        np.stack([np.stack([cosine, sine_part], 1), np.stack([-sine_part, cosine], 1)], 0)
        / length
    )
    return (forward, inverse)


def plane_tables():
    joint_index = np.arange(KZ * KT)
    depth_freq = signed_freq(KZ)[joint_index // KT]
    time_freq = joint_index % KT
    cell_index = np.arange(NZ * NT)
    turns = (
        depth_freq[:, None] * (cell_index // NT)[None, :] * NT
        + time_freq[:, None] * (cell_index % NT)[None, :] * NZ
    ) % (NZ * NT)
    angles = 2.0 * math.pi / (NZ * NT) * turns
    forward = np.stack([np.cos(angles).T, -np.sin(angles).T], 1)
    inverse = np.stack([np.cos(angles), -np.sin(angles)], 0) / (NZ * NT)
    return (forward, inverse)


def rounded_product(pattern, values, table):
    return jnp.einsum(
        pattern, values, jnp.asarray(table, jnp.bfloat16), preferred_element_type=jnp.float32
    )


def exact_product(pattern, values, table):
    return jnp.einsum(
        pattern, values, jnp.asarray(table, jnp.float32), precision=lax.Precision.HIGHEST
    )


def to_bf16(values):
    return values.astype(jnp.bfloat16)


def keep_float(values):
    return values


def exchange(values, axis):
    return lax.all_to_all(values, axis, split_axis=0, concat_axis=0, tiled=True)


def forward_modes(grad_pre, weights, tables):
    plane, first, second = tables
    rows = lax.axis_size("aa")
    columns = lax.axis_size("ba")
    plane = plane.reshape(NZ * NT, 2, rows, -1)
    spectrum = to_bf16(rounded_product("bcxyz,zpnm->nbcpxmy", grad_pre, plane))
    blocks = exchange(spectrum, "aa")
    first = first.reshape(2, rows, NX // rows, 2, columns, KX // columns)
    spectrum = to_bf16(rounded_product("nbcpxmy,pnxqgk->gbcqkmy", blocks, first))
    blocks = exchange(spectrum, "ba")
    second = second.reshape(2, columns, NY // columns, 2, KY)
    result = to_bf16(rounded_product("gbcpkmy,pgyqj->bcqkmj", blocks, second))
    shape = result.shape
    spectrum = result.reshape(shape[:4] + (shape[4] * KY,))
    real_part = spectrum[:, :, 0]
    imag_part = spectrum[:, :, 1]

    def mixing(values, matrix):
        return jnp.einsum("bokr,oikr->bikr", values, matrix, preferred_element_type=jnp.float32)

    result_real = mixing(real_part, weights[0]) + mixing(imag_part, weights[1])
    result_imag = mixing(imag_part, weights[0]) - mixing(real_part, weights[1])
    return jnp.stack([result_real, result_imag], 2)


def back_path(mode_values, tables, multiply, finish):
    first, second, plane = tables
    rows = lax.axis_size("aa")
    columns = lax.axis_size("ba")
    extent = mode_values.shape
    gridded = mode_values.reshape(extent[:4] + (extent[4] // KY, KY))
    second = second.reshape(2, KY, 2, columns, NY // columns)
    blocks = exchange(finish(multiply("bcpkmj,pjqgu->gbcqkmu", gridded, second)), "ba")
    first = first.reshape(2, columns, KX // columns, 2, rows, NX // rows)
    back = to_bf16(multiply("gbcpkmu,pgkqnx->nbcqxmu", blocks, first))
    blocks = exchange(back, "aa")
    plane = plane.reshape(2, rows, -1, NZ * NT)
    return rounded_product("nbcpxmu,pnmz->bcxuz", blocks, plane)


def per_device(cotangent, pre_activations, spectral_weights, skip_weights, lift_weights):
    plane_forward, plane_inverse = plane_tables()
    first_forward, first_inverse = line_tables(KX, NX)
    second_forward, second_inverse = line_tables(KY, NY)
    forward_tables = (plane_forward, first_forward, second_forward)
    back_tables = (first_inverse, second_inverse, plane_inverse)
    incoming = cotangent.astype(jnp.float32)
    layers = pre_activations.shape[0]
    perm_grad = None
    for layer_index in range(layers - 1, -1, -1):
        slope = gelu_slope(pre_activations[layer_index].astype(jnp.float32))
        grad_pre = (incoming * slope).astype(jnp.bfloat16)
        mode_values = forward_modes(grad_pre, spectral_weights[layer_index], forward_tables)
        if layer_index > 0:
            skip_term = jnp.einsum(
                "boxyz,oi->bixyz",
                grad_pre,
                skip_weights[layer_index],
                preferred_element_type=jnp.float32,
            )
            spectral = back_path(
                mode_values.astype(jnp.bfloat16), back_tables, rounded_product, to_bf16
            )
            incoming = skip_term + spectral
        else:
            folded = jnp.sum(mode_values * lift_weights[None, :, None, None, None], 1)[:, None]
            spectral = back_path(folded, back_tables, exact_product, keep_float)
            combined = jnp.sum(skip_weights[0].astype(jnp.float32) * lift_weights[None, :], 1)
            projected = jnp.sum(
                grad_pre.astype(jnp.float32) * combined[None, :, None, None, None], 1
            )
            perm_grad = projected + spectral[:, 0]
    return perm_grad


def solution(mesh):
    return jax.shard_map(
        per_device,
        mesh=mesh,
        in_specs=(
            P(None, None, "aa", "ba", None),
            P(None, None, None, "aa", "ba", None),
            P(None, None, None, None, "ba", "aa"),
            P(),
            P(),
        ),
        out_specs=P(None, "aa", "ba", None),
        check_vma=False,
    )
```
